32 devices in a mesh: gx: 8 (over z, x), gy: 4 (over y, core).
Axes of the slice: x: 2, y: 2, z: 4, core: 2. Of those that a mesh axis runs over, the one named last changes fastest.
Arguments:
- source: float32 [128, 64, 256], P('gx', 'gy'), may hold values from -8 to 8
- conductivity: float32 [128, 64, 256], P('gx', 'gy'), may hold values from 0.25 to 8
- reaction: float32 [128, 64, 256], P('gx', 'gy'), may hold values from 0.02 to 0.2
Outputs:
- solution: float32 [128, 64, 256], P('gx', 'gy')
The draws below stay inside these ranges and needn't reach their ends.
All inputs are finite; a program needn't handle non-finite values.
Results may differ from the reference program's by a relative error of at most 0.0003.
Values sent between devices are 32-bit elements; how exact they have to be, the bound alone decides.
A program may use at most 128 MiB of HBM per device.

```python
import math
import jax
import jax.numpy as jnp

LEVELS = 5
DEGREE = 4
BOTTOM = 8
NX = 128
NY = 64
NZ = 256


def draw_source(key, part):
    values = jax.random.normal(key, (NX, NY, NZ), jnp.float32)
    return jnp.clip(values, -8.0, 8.0)


def level_of(stream_key, dims, shards, least, high):
    def one(axis_at, shards_of):
        draws = jax.random.uniform(jax.random.fold_in(jax.random.fold_in(stream_key, 6), axis_at), (shards_of,), jnp.float32, least / len(shards), high / len(shards))
        return jnp.repeat(jnp.exp(draws), dims[axis_at] // shards_of).reshape((-1,) + (1,) * (len(dims) - axis_at - 1))

    gain = one(*shards[0])
    for cut in shards[1:]:
        gain = gain * one(*cut)
    return gain


def setup_inputs(seed: int = 0) -> dict:
    key_of = jax.random.split(jax.random.key(seed), 4)
    return {
        "source": draw_source(jax.random.fold_in(key_of[3], 71), 0),
        "conductivity": jnp.clip(jnp.exp(math.log(8.0) - 3.465736 * jax.random.uniform(key_of[1], (NX, NY, NZ), jnp.float32) ** level_of(key_of[1], (NX, NY, NZ), ((0, 8), (1, 4)), -0.2, 0.2)), 0.25, 8.0),
        "reaction": jnp.clip(jnp.exp(math.log(0.2) - 2.3025851 * jax.random.uniform(key_of[2], (NX, NY, NZ), jnp.float32) ** level_of(key_of[2], (NX, NY, NZ), ((0, 8), (1, 4)), -0.2, 0.2)), 0.02, 0.2),
    }


SMOOTH_LOWER = 0.5
SMOOTH_UPPER = 2.0
BOTTOM_LOWER = 0.02


def pad_plane(field):
    return jnp.pad(field, ((1, 1), (1, 1), (0, 0)))


def coarsen(field):
    count_a, count_b, count_c = field.shape
    return field.reshape(count_a // 2, 2, count_b // 2, 2, count_c // 2, 2).mean(axis=(1, 3, 5))


def refine(field):
    count_a, count_b, count_c = field.shape
    spread = jnp.broadcast_to(field[:, None, :, None, :, None], (count_a, 2, count_b, 2, count_c, 2))
    return spread.reshape(2 * count_a, 2 * count_b, 2 * count_c)


def face_terms(padded_coef, grid_scale):
    inner = padded_coef[1:-1, 1:-1]
    face_first = grid_scale * (0.5 * (padded_coef[:-1, 1:-1] + padded_coef[1:, 1:-1]))
    face_second = grid_scale * (0.5 * (padded_coef[1:-1, :-1] + padded_coef[1:-1, 1:]))
    z_padded = jnp.pad(inner, ((0, 0), (0, 0), (1, 1)))
    face_third = grid_scale * (0.5 * (z_padded[..., :-1] + z_padded[..., 1:]))
    return face_first, face_second, face_third


def operate(field, faces, diagonal, extend):
    face_first, face_second, face_third = faces
    padded = extend(field)
    z_padded = jnp.pad(field, ((0, 0), (0, 0), (1, 1)))
    beside = face_first[1:] * padded[2:, 1:-1] + face_first[:-1] * padded[:-2, 1:-1]
    beside = beside + face_second[:, 1:] * padded[1:-1, 2:] + face_second[:, :-1] * padded[1:-1, :-2]
    beside = beside + face_third[..., 1:] * z_padded[..., 2:] + face_third[..., :-1] * z_padded[..., :-2]
    return diagonal * field - beside


def smooth(apply_fn, diagonal, source, guess, lower, upper, count):
    center = 0.5 * (upper + lower)
    half_width = 0.5 * (upper - lower)
    quotient = center / half_width
    momentum = 1.0 / quotient
    if guess is None:
        residual = source
        guess = jnp.zeros_like(source)
    else:
        residual = source - apply_fn(guess)
    update = residual / diagonal / center
    guess = guess + update
    for iteration in range(1, count):
        residual = source - apply_fn(guess)
        momentum_new = 1.0 / (2.0 * quotient - momentum)
        update = (momentum_new * momentum) * update + (2.0 * momentum_new / half_width) * (residual / diagonal)
        guess = guess + update
        momentum = momentum_new
    return guess


def descend(grid_level, source, conductivity, reaction, extend_field, extend_coef, deeper):
    grid_scale = 0.25 ** grid_level
    faces = face_terms(extend_coef(conductivity), grid_scale)
    face_first, face_second, face_third = faces
    diagonal = reaction + face_first[1:] + face_first[:-1] + face_second[:, 1:] + face_second[:, :-1] + face_third[..., 1:] + face_third[..., :-1]

    def apply_fn(field):
        return operate(field, faces, diagonal, extend_field)

    if grid_level == LEVELS - 1:
        return smooth(apply_fn, diagonal, source, None, BOTTOM_LOWER, SMOOTH_UPPER, BOTTOM)
    guess = smooth(apply_fn, diagonal, source, None, SMOOTH_LOWER, SMOOTH_UPPER, DEGREE)
    residual = source - apply_fn(guess)
    correction = deeper(grid_level + 1, coarsen(residual), coarsen(conductivity), coarsen(reaction))
    guess = guess + refine(correction)
    return smooth(apply_fn, diagonal, source, guess, SMOOTH_LOWER, SMOOTH_UPPER, DEGREE)


def replicated(grid_level, source, conductivity, reaction):
    return descend(grid_level, source, conductivity, reaction, pad_plane, pad_plane, replicated)


def reference(source, conductivity, reaction):
    return replicated(0, source, conductivity, reaction)
```

```python
import functools

import jax
import jax.numpy as jnp
from jax import lax
from jax.experimental import pallas as pl
from jax.experimental.pallas import tpu as pltpu
from jax.sharding import PartitionSpec as P

DEGREE = 4
BOTTOM = 8
SMOOTH_LOWER = 0.5
SMOOTH_UPPER = 2.0
BOTTOM_LOWER = 0.02

MESH = pl.DeviceIdType.MESH
F32 = jnp.float32
H = 4
DIRS = [(dx, dy) for dx in (-1, 0, 1) for dy in (-1, 0, 1) if (dx, dy) != (0, 0)]


def steps(lower, upper, count):
    center, half = 0.5 * (upper + lower), 0.5 * (upper - lower)
    q = center / half
    p = 1.0 / q
    out = [(0.0, 1.0 / center)]
    for _ in range(1, count):
        pn = 1.0 / (2.0 * q - p)
        out.append((pn * p, 2.0 * pn / half))
        p = pn
    return out


def loop(lo, hi, body, unroll=1):
    def step(i, carry):
        body(i)
        return carry

    lax.fori_loop(lo, hi, step, 0, unroll=unroll)


def split_dot(v, m):
    hi = v.astype(jnp.bfloat16)
    lo = (v - hi.astype(F32)).astype(jnp.bfloat16)
    return jnp.dot(hi, m, preferred_element_type=F32) + jnp.dot(lo, m, preferred_element_type=F32)


def down_matrix(n):
    row = lax.broadcasted_iota(jnp.int32, (n, 128), 0)
    col = lax.broadcasted_iota(jnp.int32, (n, 128), 1)
    return jnp.where((row >= 2 * col) & (row < 2 * col + 2), 0.125, 0.0).astype(jnp.bfloat16)


def up_matrix(n):
    row = lax.broadcasted_iota(jnp.int32, (128, n), 0)
    col = lax.broadcasted_iota(jnp.int32, (128, n), 1)
    return jnp.where((col >= 2 * row) & (col < 2 * row + 2), 1.0, 0.0).astype(jnp.bfloat16)


class Level:
    def __init__(self, number, refs):
        self.s = 0.25**number
        self.f, self.b, self.c, self.x0, self.x1, self.d, self.g, self.inv, self.diag, self.w = refs
        self.nx, self.ny, self.nz = self.f.shape

    def zero(self, *refs):
        z = jnp.zeros((self.ny, self.nz), F32)

        def body(i):
            for r in refs:
                r[i] = z

        loop(0, self.nx, body)

    def setup(self, lo, hi):
        ny, nz = self.ny, self.nz
        row = lax.broadcasted_iota(jnp.int32, (ny, nz), 0)
        col = lax.broadcasted_iota(jnp.int32, (ny, nz), 1)
        edges = (row == 0, row == ny - 1, col == 0, col == nz - 1)

        def body(i):
            b = self.b[i]
            c = self.c[i]
            near = [
                self.b[i - 1],
                self.b[i + 1],
                jnp.where(edges[0], 0.0, pltpu.roll(b, 1, 0)),
                jnp.where(edges[1], 0.0, pltpu.roll(b, ny - 1, 0)),
                jnp.where(edges[2], 0.0, pltpu.roll(b, 1, 1)),
                jnp.where(edges[3], 0.0, pltpu.roll(b, nz - 1, 1)),
            ]
            half = 0.5 * self.s
            faces = [half * (b + n) for n in near]
            diag = c
            for face in faces:
                diag = diag + face
            inside = c > 0.0
            inv = jnp.where(inside, 1.0 / jnp.where(inside, diag, 1.0), 0.0)
            self.inv[i] = inv
            self.diag[i] = diag
            for k, face in enumerate(faces):
                w = face * inv
                if k >= 2:
                    w = jnp.where(edges[k - 2], 0.0, w)
                self.w[k, i] = w

        loop(lo, hi, body)

    def start(self, lo, hi, b):
        def body(i):
            g = self.f[i] * self.inv[i]
            self.g[i] = g
            d = g * b
            self.d[i] = d
            self.x0[i] = d

        loop(lo, hi, body)

    def scale_source(self, lo, hi):
        def body(i):
            self.g[i] = self.f[i] * self.inv[i]

        loop(lo, hi, body)

    def scaled_residual(self, x, i):
        v = x[i]
        t = self.g[i] - v
        t = t + self.w[0, i] * x[i - 1] + self.w[1, i] * x[i + 1]
        t = t + self.w[2, i] * pltpu.roll(v, 1, 0) + self.w[3, i] * pltpu.roll(v, self.ny - 1, 0)
        t = t + self.w[4, i] * pltpu.roll(v, 1, 1) + self.w[5, i] * pltpu.roll(v, self.nz - 1, 1)
        return v, t

    def sweep(self, x, y, a, b, lo, hi):
        def body(i):
            v, t = self.scaled_residual(x, i)
            d = b * t
            if a != 0.0:
                d = a * self.d[i] + d
            self.d[i] = d
            y[i] = v + d

        loop(lo, hi, body)

    def pre(self, lo, hi, shrink, pairs):
        self.start(lo, hi, pairs[0][1])
        x, y = self.x0, self.x1
        for a, b in pairs[1:]:
            lo, hi = lo + shrink, hi - shrink
            self.sweep(x, y, a, b, lo, hi)
            x, y = y, x
        return x, y

    def post(self, x, y, lo, hi, shrink, pairs):
        for a, b in pairs:
            lo, hi = lo + shrink, hi - shrink
            self.sweep(x, y, a, b, lo, hi)
            x, y = y, x
        return x, y

    def coarse_residual(self, x, first, count, m, scratch):
        def body(i):
            j = first + 2 * i
            _, t0 = self.scaled_residual(x, j)
            _, t1 = self.scaled_residual(x, j + 1)
            v = self.diag[j] * t0 + self.diag[j + 1] * t1
            scratch[i * self.ny : (i + 1) * self.ny, :] = split_dot(v, m)

        for i in range(count):
            body(i)


def coarse_array(ref, first, count, m, scratch):
    ny = ref.shape[1]
    for i in range(count):
        v = ref[first + 2 * i] + ref[first + 2 * i + 1]
        scratch[i * ny : (i + 1) * ny, :] = split_dot(v, m)


def pairs_of(scratch, start, size):
    return scratch[pl.ds(start, size, stride=2), :] + scratch[pl.ds(start + 1, size, stride=2), :]


def kernel(
    nx_dev, ny_dev, f_in, b_in, c_in, out, *refs
):
    refs = list(refs)

    def take(n):
        got = refs[:n]
        del refs[:n]
        return got

    levels = [Level(k, take(10)) for k in range(5)]
    l0, l1, l2, l3, l4 = levels
    scratch, e2pad, f2s, bc2s, f2l, bc2l = take(6)
    sx, sy, sc, rx, ry, rc = take(6)
    tx, ty, tc, ux, uy, uc = take(6)
    bc1s, bc1r, f1s, f1r, x1s, x1r = take(6)
    ssem, rsem, gssem, grsem = take(4)

    gx = lax.axis_index("gx")
    gy = lax.axis_index("gy")
    n = nx_dev * ny_dev
    me = gx * ny_dev + gy
    m256, m128 = down_matrix(256), down_matrix(128)
    u256, u128 = up_matrix(256), up_matrix(128)

    barrier = pltpu.get_barrier_semaphore()

    def greet(k):
        t = lax.rem(me + k, n)
        pl.semaphore_signal(
            barrier, inc=1, device_id=(t // ny_dev, lax.rem(t, ny_dev)), device_id_type=MESH
        )

    loop(1, n, greet)

    def present(dx, dy):
        ok = None
        for delta, at, size in ((dx, gx, nx_dev), (dy, gy, ny_dev)):
            if delta == 1:
                cond = at < size - 1
            elif delta == -1:
                cond = at > 0
            else:
                continue
            ok = cond if ok is None else ok & cond
        return ok

    def neighbour_copy(k, turn, src, dst):
        dx, dy = DIRS[k]
        return pltpu.make_async_remote_copy(
            src_ref=src,
            dst_ref=dst,
            send_sem=ssem.at[turn, k],
            recv_sem=rsem.at[turn, k],
            device_id=(gx + dx, gy + dy),
            device_id_type=MESH,
        )

    def slot(k, xs, ys, cs):
        dx, dy = DIRS[k]
        if dy == 0:
            return xs.at[(dx + 1) // 2]
        if dx == 0:
            return ys.at[(dy + 1) // 2]
        return cs.at[(dx + 1) + (dy + 1) // 2]

    def send_all(turn, pair_of):
        for k, (dx, dy) in enumerate(DIRS):

            @pl.when(present(dx, dy))
            def _():
                neighbour_copy(k, turn, *pair_of(k)).start()

    def arrive_all(turn, pair_of, use):
        for k, (dx, dy) in enumerate(DIRS):

            @pl.when(present(-dx, -dy))
            def _():
                neighbour_copy(k, turn, *pair_of(k)).wait_recv()
                use(k, dx, dy)

    def sent_all(turn, pair_of):
        for k, (dx, dy) in enumerate(DIRS):

            @pl.when(present(dx, dy))
            def _():
                neighbour_copy(k, turn, *pair_of(k)).wait_send()

    def source_span(delta):
        if delta == 0:
            return 0, 16, None, None
        return (16 - H, H, 16 - H, 15 - H) if delta == 1 else (0, H, H - 1, H)

    def landing(delta):
        return {0: (H, 16), 1: (0, H), -1: (H + 16, H)}[delta]

    for k, (dx, dy) in enumerate(DIRS):
        buf = slot(k, sx, sy, sc)
        px, cx, ox, beyx = source_span(dx)
        py, cy, oy, beyy = source_span(dy)
        for which, ref in enumerate((f_in, b_in, c_in)):

            def body(i, which=which, ref=ref, buf=buf, px=px, py=py, cy=cy):
                buf[which, i] = ref[px + i, py : py + cy, :]

            loop(0, cx, body)
        if dx != 0:
            i = ox - px
            buf[2, i] = buf[2, i] + 0.5 * b_in[beyx, py : py + cy, :]
        if dy != 0:

            def edge(i, buf=buf, px=px, py=py, oy=oy, beyy=beyy):
                buf[2, i, oy - py : oy - py + 1, :] = (
                    buf[2, i, oy - py : oy - py + 1, :] + 0.5 * b_in[px + i, beyy : beyy + 1, :]
                )

            loop(0, cx, edge)

    bc1 = []
    for which, ref in enumerate((b_in, c_in)):
        coarse_array(ref, 0, 8, m256, scratch)
        for i in range(8):
            bc1s[which, i] = pairs_of(scratch, 16 * i, 8)
    half = []
    for which in range(2):
        coarse_array(bc1s.at[which], 0, 4, m128, scratch)
        half.append(
            jnp.concatenate([pairs_of(scratch, 8 * i, 4) for i in range(4)], axis=0)
        )
    bc2s[...] = half[0] + pltpu.roll(half[1], 64, 1)

    pl.semaphore_wait(barrier, n - 1)

    strips = lambda k: (slot(k, sx, sy, sc), slot(k, rx, ry, rc))
    bricks = lambda s, r: (lambda k: (s, r.at[k]))
    send_all(0, strips)
    send_all(1, bricks(bc1s, bc1r))

    def gather_start(turn, src, dst):
        dst[me] = src[...]

        def body(k):
            t = lax.rem(me + k, n)
            pltpu.make_async_remote_copy(
                src_ref=src,
                dst_ref=dst.at[me],
                send_sem=gssem.at[turn],
                recv_sem=grsem.at[turn],
                device_id=(t // ny_dev, lax.rem(t, ny_dev)),
                device_id_type=MESH,
            ).start()

        loop(1, n, body)

    def gather_wait(turn, dst):
        whole = dst.at[pl.ds(0, n - 1)]
        other = lax.rem(me + 1, n)
        copy = pltpu.make_async_remote_copy(
            src_ref=whole,
            dst_ref=whole,
            send_sem=gssem.at[turn],
            recv_sem=grsem.at[turn],
            device_id=(other // ny_dev, lax.rem(other, ny_dev)),
            device_id_type=MESH,
        )
        copy.wait_send()
        copy.wait_recv()

    gather_start(0, bc2s, bc2l)

    l0.zero(l0.f, l0.b, l0.c)

    def inner(i):
        for dst, src in ((l0.f, f_in), (l0.b, b_in), (l0.c, c_in)):
            dst[i + 1 + H, H : H + 16, :] = src[i]

    loop(0, 16, inner)

    def place(dsts, xs, ys, cs):
        def use(k, dx, dy):
            buf = slot(k, xs, ys, cs)
            px, cx = landing(dx)
            py, cy = landing(dy)

            def body(i):
                for which, dst in enumerate(dsts):
                    dst[1 + px + i, py : py + cy, :] = buf[which, i]

            loop(0, cx, body)

        return use

    arrive_all(0, strips, place((l0.f, l0.b, l0.c), rx, ry, rc))
    l0.setup(1, 25)
    x0, y0 = l0.pre(1, 25, 1, steps(SMOOTH_LOWER, SMOOTH_UPPER, DEGREE))
    l0.coarse_residual(x0, 1 + H, 8, m256, scratch)
    for i in range(8):
        f1s[i] = pairs_of(scratch, 24 * i + H, 8)
    send_all(2, bricks(f1s, f1r))

    for k, (dx, dy) in enumerate(DIRS):
        buf = slot(k, tx, ty, tc)
        px, cx, _, _ = source_span(dx)
        py, cy, _, _ = source_span(dy)

        def body(i, buf=buf, px=px, py=py, cy=cy):
            buf[0, i] = x0[1 + H + px + i, H + py : H + py + cy, :]

        loop(0, cx, body)
    xstrips = lambda k: (slot(k, tx, ty, tc), slot(k, ux, uy, uc))

    l1.zero(l1.f, l1.b, l1.c)

    def brick(dsts, src):
        def use(k, dx, dy):
            for which, dst in enumerate(dsts):
                for i in range(8):
                    dst[9 - 8 * dx + i, 8 - 8 * dy : 16 - 8 * dy, :] = src(k, which, i)

        return use

    for i in range(8):
        l1.b[9 + i, 8:16, :] = bc1s[0, i]
        l1.c[9 + i, 8:16, :] = bc1s[1, i]
        l1.f[9 + i, 8:16, :] = f1s[i]
    arrive_all(1, bricks(bc1s, bc1r), brick((l1.b, l1.c), lambda k, w, i: bc1r[k, w, i]))
    l1.setup(1, 25)
    arrive_all(2, bricks(f1s, f1r), brick((l1.f,), lambda k, w, i: f1r[k, i]))
    x1, y1 = l1.pre(1, 25, 1, steps(SMOOTH_LOWER, SMOOTH_UPPER, DEGREE))
    l1.coarse_residual(x1, 9, 4, m128, scratch)
    f2 = [pairs_of(scratch, 24 * i + 8, 4) for i in range(4)]
    f2s[...] = jnp.concatenate(f2[:2], axis=0) + pltpu.roll(
        jnp.concatenate(f2[2:], axis=0), 64, 1
    )
    gather_start(1, f2s, f2l)
    for i in range(8):
        x1s[i] = x1[9 + i, 8:16, :]
    send_all(3, bricks(x1s, x1r))
    send_all(4, xstrips)

    for lv in (l2, l3, l4):
        lv.zero(lv.f, lv.b, lv.c, lv.x0, lv.x1)
    gather_wait(0, bc2l)

    def low(v):
        col = lax.broadcasted_iota(jnp.int32, v.shape, 1)
        return jnp.where(col < 64, v, 0.0)

    def spread_bc(a):
        for e in range(ny_dev):
            v = bc2l[a * ny_dev + e]
            b2, c2 = low(v), low(pltpu.roll(v, 64, 1))
            for i in range(4):
                l2.b[1 + 4 * a + i, 4 * e : 4 * e + 4, :] = b2[4 * i : 4 * i + 4]
                l2.c[1 + 4 * a + i, 4 * e : 4 * e + 4, :] = c2[4 * i : 4 * i + 4]

    loop(0, nx_dev, spread_bc)
    for fine, coarse in ((l2, l3), (l3, l4)):
        nxc, nyc = (fine.nx - 2) // 2, fine.ny // 2
        for src, dst in ((fine.b, coarse.b), (fine.c, coarse.c)):
            coarse_array(src, 1, nxc, m128, scratch)
            for i in range(nxc):
                dst[1 + i, 0:nyc, :] = pairs_of(scratch, fine.ny * i, nyc)
    for lv in (l2, l3, l4):
        lv.setup(1, lv.nx - 1)

    gather_wait(1, f2l)

    def spread_f(a):
        for e in range(ny_dev):
            v = f2l[a * ny_dev + e]
            p01, p23 = low(v), low(pltpu.roll(v, 64, 1))
            for i in range(4):
                p = (p01, p23)[i // 2]
                r = 4 * (i % 2)
                l2.f[1 + 4 * a + i, 4 * e : 4 * e + 4, :] = p[r : r + 4]

    loop(0, nx_dev, spread_f)
    found = []
    for fine, coarse in ((l2, l3), (l3, l4)):
        x, y = fine.pre(1, fine.nx - 1, 0, steps(SMOOTH_LOWER, SMOOTH_UPPER, DEGREE))
        found.append((x, y))
        nxc, nyc = (fine.nx - 2) // 2, fine.ny // 2
        fine.coarse_residual(x, 1, nxc, m128, scratch)
        for i in range(nxc):
            coarse.f[1 + i, 0:nyc, :] = pairs_of(scratch, fine.ny * i, nyc)
    e, _ = l4.pre(1, l4.nx - 1, 0, steps(BOTTOM_LOWER, SMOOTH_UPPER, BOTTOM))

    def refine_plane(v, rows, at, u):
        scratch[pl.ds(at, rows, stride=2), :] = v
        scratch[pl.ds(at + 1, rows, stride=2), :] = v
        return split_dot(scratch[at : at + 2 * rows, :], u)

    for fine, coarse, (x, y) in ((l3, l4, found[1]), (l2, l3, found[0])):
        nxc, nyc = (fine.nx - 2) // 2, fine.ny // 2
        for i in range(nxc):
            up = refine_plane(e[1 + i][0:nyc], nyc, i * fine.ny, u128)
            x[1 + 2 * i] = x[1 + 2 * i] + up
            x[2 + 2 * i] = x[2 + 2 * i] + up
        e, _ = fine.post(x, y, 1, fine.nx - 1, 0, steps(SMOOTH_LOWER, SMOOTH_UPPER, DEGREE))

    yt = e2pad.shape[1]
    zero_plane = jnp.zeros((yt, 128), F32)

    def clear(i):
        e2pad[i] = zero_plane

    loop(0, e2pad.shape[0], clear)

    def pad_e2(i):
        e2pad[4 + i, 4 : 4 + l2.ny, :] = e[1 + i]

    loop(0, l2.nx - 2, pad_e2)
    arrive_all(3, bricks(x1s, x1r), brick((x1,), lambda k, w, i: x1r[k, i]))

    def add(fine, x, j, up):
        x[j] = jnp.where(fine.inv[j] > 0.0, x[j] + up, 0.0)

    turn_by = lax.rem(yt - 4 * gy, yt)
    for i in range(12):
        v = pltpu.roll(e2pad[4 * gx + i], turn_by, 0)[0:12]
        up = refine_plane(v, 12, 24 * i, u128)
        add(l1, x1, 1 + 2 * i, up)
        add(l1, x1, 2 + 2 * i, up)
    e1, _ = l1.post(x1, y1, 3, 23, 1, steps(SMOOTH_LOWER, SMOOTH_UPPER, DEGREE))

    arrive_all(4, xstrips, place((x0,), ux, uy, uc))
    for i in range(12):
        up = refine_plane(e1[7 + i][6:18], 12, 24 * i, u256)
        add(l0, x0, 1 + 2 * i, up)
        add(l0, x0, 2 + 2 * i, up)
    r0, _ = l0.post(x0, y0, 1, 25, 1, steps(SMOOTH_LOWER, SMOOTH_UPPER, DEGREE))

    def give(i):
        out[i] = r0[1 + H + i, H : H + 16, :]

    loop(0, 16, give)
    sent_all(0, strips)
    sent_all(1, bricks(bc1s, bc1r))
    sent_all(2, bricks(f1s, f1r))
    sent_all(3, bricks(x1s, x1r))
    sent_all(4, xstrips)


def solution(mesh):
    nx_dev, ny_dev = mesh.shape["gx"], mesh.shape["gy"]
    n = nx_dev * ny_dev
    y2 = 4 * ny_dev

    def vm(*shape):
        return pltpu.VMEM(shape, F32)

    dims = [(26, 24, 256), (26, 24, 128)]
    for k in range(3):
        dims.append((2 + (4 * nx_dev >> k), max(8, y2 >> k), 128))
    shapes = []
    for d in dims:
        shapes += [vm(*d)] * 9 + [vm(6, *d)]
    shapes += [
        vm(max(12 * 24, 2 * nx_dev * y2), 128),
        vm(4 * nx_dev + 8, y2 + 8, 128),
        vm(8, 128),
        vm(16, 128),
        vm(n, 8, 128),
        vm(n, 16, 128),
    ]
    for count in (3, 3, 1, 1):
        shapes += [
            vm(2, count, H, 16, 256),
            vm(2, count, 16, H, 256),
            vm(4, count, H, H, 256),
        ]
    shapes += [vm(2, 8, 8, 128), vm(8, 2, 8, 8, 128)]
    shapes += [vm(8, 8, 128), vm(8, 8, 8, 128)] * 2
    shapes += [
        pltpu.SemaphoreType.DMA((5, 8)),
        pltpu.SemaphoreType.DMA((5, 8)),
        pltpu.SemaphoreType.DMA((2,)),
        pltpu.SemaphoreType.DMA((2,)),
    ]

    def per_device(source, conductivity, reaction):
        return pl.pallas_call(
            functools.partial(kernel, nx_dev, ny_dev),
            out_shape=jax.ShapeDtypeStruct(source.shape, F32),
            in_specs=[pl.BlockSpec(memory_space=pltpu.VMEM)] * 3,
            out_specs=pl.BlockSpec(memory_space=pltpu.VMEM),
            scratch_shapes=shapes,
            compiler_params=pltpu.CompilerParams(
                collective_id=0, has_side_effects=True, vmem_limit_bytes=48 << 20
            ),
        )(source, conductivity, reaction)

    spec = P("gx", "gy", None)
    return jax.shard_map(
        per_device, mesh=mesh, in_specs=(spec,) * 3, out_specs=spec, check_vma=False
    )
```

```python
import functools

import jax
import jax.numpy as jnp
from jax import lax
from jax.experimental import pallas as pl
from jax.experimental.pallas import tpu as pltpu
from jax.sharding import PartitionSpec as P

DEGREE = 4
BOTTOM = 8
SMOOTH_LOWER = 0.5
SMOOTH_UPPER = 2.0
BOTTOM_LOWER = 0.02

MESH = pl.DeviceIdType.MESH
F32 = jnp.float32
H = 4
DIRS = [(dx, dy) for dx in (-1, 0, 1) for dy in (-1, 0, 1) if (dx, dy) != (0, 0)]


def steps(lower, upper, count):
    center, half = 0.5 * (upper + lower), 0.5 * (upper - lower)
    q = center / half
    p = 1.0 / q
    out = [(0.0, 1.0 / center)]
    for _ in range(1, count):
        pn = 1.0 / (2.0 * q - p)
        out.append((pn * p, 2.0 * pn / half))
        p = pn
    return out


def loop(lo, hi, body, unroll=1):
    def step(i, carry):
        body(i)
        return carry

    lax.fori_loop(lo, hi, step, 0, unroll=unroll)


def planes(lo, hi, body, chunk):
    chunk = min(chunk, hi - lo)

    def group(i, size):
        stores = []
        for k in range(size):
            stores += body(i + k)
        for ref, index, value in stores:
            ref[index] = value

    whole = (hi - lo) // chunk
    if whole == 1:
        group(lo, chunk)
    else:
        loop(0, whole, lambda j: group(lo + j * chunk, chunk))
    if whole * chunk < hi - lo:
        group(lo + whole * chunk, hi - lo - whole * chunk)


def split_dot(v, m):
    hi = v.astype(jnp.bfloat16)
    lo = (v - hi.astype(F32)).astype(jnp.bfloat16)
    return jnp.dot(hi, m, preferred_element_type=F32) + jnp.dot(lo, m, preferred_element_type=F32)


def down_matrix(n):
    row = lax.broadcasted_iota(jnp.int32, (n, 128), 0)
    col = lax.broadcasted_iota(jnp.int32, (n, 128), 1)
    return jnp.where((row >= 2 * col) & (row < 2 * col + 2), 0.125, 0.0).astype(jnp.bfloat16)


def up_matrix(n):
    row = lax.broadcasted_iota(jnp.int32, (128, n), 0)
    col = lax.broadcasted_iota(jnp.int32, (128, n), 1)
    return jnp.where((col >= 2 * row) & (col < 2 * row + 2), 1.0, 0.0).astype(jnp.bfloat16)


class Level:
    def __init__(self, number, refs):
        self.s = 0.25**number
        self.f, self.b, self.c, self.x0, self.x1, self.d, self.g, self.inv, self.diag, self.w = refs
        self.nx, self.ny, self.nz = self.f.shape
        vregs = self.ny * self.nz // 1024
        self.chunk = max(2, 16 // vregs)

    def zero(self, *refs):
        z = jnp.zeros((self.ny, self.nz), F32)

        planes(0, self.nx, lambda i: [(r, i, z) for r in refs], self.chunk)

    def setup(self, lo, hi):
        ny, nz = self.ny, self.nz
        row = lax.broadcasted_iota(jnp.int32, (ny, nz), 0)
        col = lax.broadcasted_iota(jnp.int32, (ny, nz), 1)
        edges = (row == 0, row == ny - 1, col == 0, col == nz - 1)

        def body(i):
            b = self.b[i]
            c = self.c[i]
            near = [
                self.b[i - 1],
                self.b[i + 1],
                jnp.where(edges[0], 0.0, pltpu.roll(b, 1, 0)),
                jnp.where(edges[1], 0.0, pltpu.roll(b, ny - 1, 0)),
                jnp.where(edges[2], 0.0, pltpu.roll(b, 1, 1)),
                jnp.where(edges[3], 0.0, pltpu.roll(b, nz - 1, 1)),
            ]
            half = 0.5 * self.s
            faces = [half * (b + n) for n in near]
            diag = c
            for face in faces:
                diag = diag + face
            inside = c > 0.0
            inv = jnp.where(inside, 1.0 / jnp.where(inside, diag, 1.0), 0.0)
            stores = [(self.inv, i, inv), (self.diag, i, diag)]
            for k, face in enumerate(faces):
                w = face * inv
                if k >= 2:
                    w = jnp.where(edges[k - 2], 0.0, w)
                stores.append((self.w, (k, i), w))
            return stores

        planes(lo, hi, body, self.chunk)

    def start(self, lo, hi, b):
        def body(i):
            g = self.f[i] * self.inv[i]
            d = g * b
            return [(self.g, i, g), (self.d, i, d), (self.x0, i, d)]

        planes(lo, hi, body, self.chunk)

    def scaled_residual(self, x, i):
        v = x[i]
        t = self.g[i] - v
        t = t + self.w[0, i] * x[i - 1] + self.w[1, i] * x[i + 1]
        t = t + self.w[2, i] * pltpu.roll(v, 1, 0) + self.w[3, i] * pltpu.roll(v, self.ny - 1, 0)
        t = t + self.w[4, i] * pltpu.roll(v, 1, 1) + self.w[5, i] * pltpu.roll(v, self.nz - 1, 1)
        return v, t

    def sweep(self, x, y, a, b, lo, hi):
        def body(i):
            v, t = self.scaled_residual(x, i)
            d = b * t
            if a != 0.0:
                d = a * self.d[i] + d
            return [(self.d, i, d), (y, i, v + d)]

        planes(lo, hi, body, self.chunk)

    def pre(self, lo, hi, shrink, pairs):
        self.start(lo, hi, pairs[0][1])
        x, y = self.x0, self.x1
        for a, b in pairs[1:]:
            lo, hi = lo + shrink, hi - shrink
            self.sweep(x, y, a, b, lo, hi)
            x, y = y, x
        return x, y

    def post(self, x, y, lo, hi, shrink, pairs):
        for a, b in pairs:
            lo, hi = lo + shrink, hi - shrink
            self.sweep(x, y, a, b, lo, hi)
            x, y = y, x
        return x, y

    def coarse_residual(self, x, first, count, m, scratch):
        def body(i):
            j = first + 2 * i
            _, t0 = self.scaled_residual(x, j)
            _, t1 = self.scaled_residual(x, j + 1)
            v = self.diag[j] * t0 + self.diag[j + 1] * t1
            scratch[i * self.ny : (i + 1) * self.ny, :] = split_dot(v, m)

        for i in range(count):
            body(i)


def coarse_array(ref, first, count, m, scratch):
    ny = ref.shape[1]
    for i in range(count):
        v = ref[first + 2 * i] + ref[first + 2 * i + 1]
        scratch[i * ny : (i + 1) * ny, :] = split_dot(v, m)


def pairs_of(scratch, start, size):
    return scratch[pl.ds(start, size, stride=2), :] + scratch[pl.ds(start + 1, size, stride=2), :]


def kernel(
    nx_dev, ny_dev, f_in, b_in, c_in, out, *refs
):
    refs = list(refs)

    def take(n):
        got = refs[:n]
        del refs[:n]
        return got

    levels = [Level(k, take(10)) for k in range(5)]
    l0, l1, l2, l3, l4 = levels
    scratch, e2pad, f2s, bc2s, f2l, bc2l = take(6)
    sx, sy, sc, rx, ry, rc = take(6)
    tx, ty, tc, ux, uy, uc = take(6)
    bc1s, bc1r, f1s, f1r, x1s, x1r = take(6)
    ssem, rsem, gssem, grsem = take(4)

    gx = lax.axis_index("gx")
    gy = lax.axis_index("gy")
    n = nx_dev * ny_dev
    me = gx * ny_dev + gy
    m256, m128 = down_matrix(256), down_matrix(128)
    u256, u128 = up_matrix(256), up_matrix(128)

    barrier = pltpu.get_barrier_semaphore()

    def greet(k):
        t = lax.rem(me + k, n)
        pl.semaphore_signal(
            barrier, inc=1, device_id=(t // ny_dev, lax.rem(t, ny_dev)), device_id_type=MESH
        )

    loop(1, n, greet)

    def present(dx, dy):
        ok = None
        for delta, at, size in ((dx, gx, nx_dev), (dy, gy, ny_dev)):
            if delta == 1:
                cond = at < size - 1
            elif delta == -1:
                cond = at > 0
            else:
                continue
            ok = cond if ok is None else ok & cond
        return ok

    def neighbour_copy(k, turn, src, dst):
        dx, dy = DIRS[k]
        return pltpu.make_async_remote_copy(
            src_ref=src,
            dst_ref=dst,
            send_sem=ssem.at[turn, k],
            recv_sem=rsem.at[turn, k],
            device_id=(gx + dx, gy + dy),
            device_id_type=MESH,
        )

    def slot(k, xs, ys, cs):
        dx, dy = DIRS[k]
        if dy == 0:
            return xs.at[(dx + 1) // 2]
        if dx == 0:
            return ys.at[(dy + 1) // 2]
        return cs.at[(dx + 1) + (dy + 1) // 2]

    def send_all(turn, pair_of):
        for k, (dx, dy) in enumerate(DIRS):

            @pl.when(present(dx, dy))
            def _():
                neighbour_copy(k, turn, *pair_of(k)).start()

    def arrive_all(turn, pair_of, use):
        for k, (dx, dy) in enumerate(DIRS):

            @pl.when(present(-dx, -dy))
            def _():
                neighbour_copy(k, turn, *pair_of(k)).wait_recv()
                use(k, dx, dy)

    def sent_all(turn, pair_of):
        for k, (dx, dy) in enumerate(DIRS):

            @pl.when(present(dx, dy))
            def _():
                neighbour_copy(k, turn, *pair_of(k)).wait_send()

    def source_span(delta):
        if delta == 0:
            return 0, 16, None, None
        return (16 - H, H, 16 - H, 15 - H) if delta == 1 else (0, H, H - 1, H)

    def landing(delta):
        return {0: (H, 16), 1: (0, H), -1: (H + 16, H)}[delta]

    for k, (dx, dy) in enumerate(DIRS):
        buf = slot(k, sx, sy, sc)
        px, cx, ox, beyx = source_span(dx)
        py, cy, oy, beyy = source_span(dy)
        for which, ref in enumerate((f_in, b_in, c_in)):

            def body(i, which=which, ref=ref, buf=buf, px=px, py=py, cy=cy):
                buf[which, i] = ref[px + i, py : py + cy, :]

            loop(0, cx, body)
        if dx != 0:
            i = ox - px
            buf[2, i] = buf[2, i] + 0.5 * b_in[beyx, py : py + cy, :]
        if dy != 0:

            def edge(i, buf=buf, px=px, py=py, oy=oy, beyy=beyy):
                buf[2, i, oy - py : oy - py + 1, :] = (
                    buf[2, i, oy - py : oy - py + 1, :] + 0.5 * b_in[px + i, beyy : beyy + 1, :]
                )

            loop(0, cx, edge)

    bc1 = []
    for which, ref in enumerate((b_in, c_in)):
        coarse_array(ref, 0, 8, m256, scratch)
        for i in range(8):
            bc1s[which, i] = pairs_of(scratch, 16 * i, 8)
    half = []
    for which in range(2):
        coarse_array(bc1s.at[which], 0, 4, m128, scratch)
        half.append(
            jnp.concatenate([pairs_of(scratch, 8 * i, 4) for i in range(4)], axis=0)
        )
    bc2s[...] = half[0] + pltpu.roll(half[1], 64, 1)

    pl.semaphore_wait(barrier, n - 1)

    strips = lambda k: (slot(k, sx, sy, sc), slot(k, rx, ry, rc))
    bricks = lambda s, r: (lambda k: (s, r.at[k]))
    send_all(0, strips)
    send_all(1, bricks(bc1s, bc1r))

    def gather_start(turn, src, dst):
        dst[me] = src[...]

        def body(k):
            t = lax.rem(me + k, n)
            pltpu.make_async_remote_copy(
                src_ref=src,
                dst_ref=dst.at[me],
                send_sem=gssem.at[turn],
                recv_sem=grsem.at[turn],
                device_id=(t // ny_dev, lax.rem(t, ny_dev)),
                device_id_type=MESH,
            ).start()

        loop(1, n, body)

    def gather_wait(turn, dst):
        whole = dst.at[pl.ds(0, n - 1)]
        other = lax.rem(me + 1, n)
        copy = pltpu.make_async_remote_copy(
            src_ref=whole,
            dst_ref=whole,
            send_sem=gssem.at[turn],
            recv_sem=grsem.at[turn],
            device_id=(other // ny_dev, lax.rem(other, ny_dev)),
            device_id_type=MESH,
        )
        copy.wait_send()
        copy.wait_recv()

    gather_start(0, bc2s, bc2l)

    l0.zero(l0.f, l0.b, l0.c)

    def inner(i):
        for dst, src in ((l0.f, f_in), (l0.b, b_in), (l0.c, c_in)):
            dst[i + 1 + H, H : H + 16, :] = src[i]

    loop(0, 16, inner)

    def place(dsts, xs, ys, cs):
        def use(k, dx, dy):
            buf = slot(k, xs, ys, cs)
            px, cx = landing(dx)
            py, cy = landing(dy)

            def body(i):
                for which, dst in enumerate(dsts):
                    dst[1 + px + i, py : py + cy, :] = buf[which, i]

            loop(0, cx, body)

        return use

    arrive_all(0, strips, place((l0.f, l0.b, l0.c), rx, ry, rc))
    l0.setup(1, 25)
    x0, y0 = l0.pre(1, 25, 1, steps(SMOOTH_LOWER, SMOOTH_UPPER, DEGREE))
    l0.coarse_residual(x0, 1 + H, 8, m256, scratch)
    for i in range(8):
        f1s[i] = pairs_of(scratch, 24 * i + H, 8)
    send_all(2, bricks(f1s, f1r))

    for k, (dx, dy) in enumerate(DIRS):
        buf = slot(k, tx, ty, tc)
        px, cx, _, _ = source_span(dx)
        py, cy, _, _ = source_span(dy)

        def body(i, buf=buf, px=px, py=py, cy=cy):
            buf[0, i] = x0[1 + H + px + i, H + py : H + py + cy, :]

        loop(0, cx, body)
    xstrips = lambda k: (slot(k, tx, ty, tc), slot(k, ux, uy, uc))

    l1.zero(l1.f, l1.b, l1.c)

    def brick(dsts, src):
        def use(k, dx, dy):
            for which, dst in enumerate(dsts):
                for i in range(8):
                    dst[9 - 8 * dx + i, 8 - 8 * dy : 16 - 8 * dy, :] = src(k, which, i)

        return use

    for i in range(8):
        l1.b[9 + i, 8:16, :] = bc1s[0, i]
        l1.c[9 + i, 8:16, :] = bc1s[1, i]
        l1.f[9 + i, 8:16, :] = f1s[i]
    arrive_all(1, bricks(bc1s, bc1r), brick((l1.b, l1.c), lambda k, w, i: bc1r[k, w, i]))
    l1.setup(1, 25)
    arrive_all(2, bricks(f1s, f1r), brick((l1.f,), lambda k, w, i: f1r[k, i]))
    x1, y1 = l1.pre(1, 25, 1, steps(SMOOTH_LOWER, SMOOTH_UPPER, DEGREE))
    l1.coarse_residual(x1, 9, 4, m128, scratch)
    f2 = [pairs_of(scratch, 24 * i + 8, 4) for i in range(4)]
    f2s[...] = jnp.concatenate(f2[:2], axis=0) + pltpu.roll(
        jnp.concatenate(f2[2:], axis=0), 64, 1
    )
    gather_start(1, f2s, f2l)
    for i in range(8):
        x1s[i] = x1[9 + i, 8:16, :]
    send_all(3, bricks(x1s, x1r))
    send_all(4, xstrips)

    for lv in (l2, l3, l4):
        lv.zero(lv.f, lv.b, lv.c, lv.x0, lv.x1)
    gather_wait(0, bc2l)

    def low(v):
        col = lax.broadcasted_iota(jnp.int32, v.shape, 1)
        return jnp.where(col < 64, v, 0.0)

    def spread_bc(a):
        for e in range(ny_dev):
            v = bc2l[a * ny_dev + e]
            b2, c2 = low(v), low(pltpu.roll(v, 64, 1))
            for i in range(4):
                l2.b[1 + 4 * a + i, 4 * e : 4 * e + 4, :] = b2[4 * i : 4 * i + 4]
                l2.c[1 + 4 * a + i, 4 * e : 4 * e + 4, :] = c2[4 * i : 4 * i + 4]

    loop(0, nx_dev, spread_bc)
    for fine, coarse in ((l2, l3), (l3, l4)):
        nxc, nyc = (fine.nx - 2) // 2, fine.ny // 2
        for src, dst in ((fine.b, coarse.b), (fine.c, coarse.c)):
            coarse_array(src, 1, nxc, m128, scratch)
            for i in range(nxc):
                dst[1 + i, 0:nyc, :] = pairs_of(scratch, fine.ny * i, nyc)
    for lv in (l2, l3, l4):
        lv.setup(1, lv.nx - 1)

    gather_wait(1, f2l)

    def spread_f(a):
        for e in range(ny_dev):
            v = f2l[a * ny_dev + e]
            p01, p23 = low(v), low(pltpu.roll(v, 64, 1))
            for i in range(4):
                p = (p01, p23)[i // 2]
                r = 4 * (i % 2)
                l2.f[1 + 4 * a + i, 4 * e : 4 * e + 4, :] = p[r : r + 4]

    loop(0, nx_dev, spread_f)
    found = []
    for fine, coarse in ((l2, l3), (l3, l4)):
        x, y = fine.pre(1, fine.nx - 1, 0, steps(SMOOTH_LOWER, SMOOTH_UPPER, DEGREE))
        found.append((x, y))
        nxc, nyc = (fine.nx - 2) // 2, fine.ny // 2
        fine.coarse_residual(x, 1, nxc, m128, scratch)
        for i in range(nxc):
            coarse.f[1 + i, 0:nyc, :] = pairs_of(scratch, fine.ny * i, nyc)
    e, _ = l4.pre(1, l4.nx - 1, 0, steps(BOTTOM_LOWER, SMOOTH_UPPER, BOTTOM))

    def refine_plane(v, rows, at, u):
        scratch[pl.ds(at, rows, stride=2), :] = v
        scratch[pl.ds(at + 1, rows, stride=2), :] = v
        return split_dot(scratch[at : at + 2 * rows, :], u)

    for fine, coarse, (x, y) in ((l3, l4, found[1]), (l2, l3, found[0])):
        nxc, nyc = (fine.nx - 2) // 2, fine.ny // 2
        for i in range(nxc):
            up = refine_plane(e[1 + i][0:nyc], nyc, i * fine.ny, u128)
            x[1 + 2 * i] = x[1 + 2 * i] + up
            x[2 + 2 * i] = x[2 + 2 * i] + up
        e, _ = fine.post(x, y, 1, fine.nx - 1, 0, steps(SMOOTH_LOWER, SMOOTH_UPPER, DEGREE))

    yt = e2pad.shape[1]
    zero_plane = jnp.zeros((yt, 128), F32)

    def clear(i):
        e2pad[i] = zero_plane

    loop(0, e2pad.shape[0], clear)

    def pad_e2(i):
        e2pad[4 + i, 4 : 4 + l2.ny, :] = e[1 + i]

    loop(0, l2.nx - 2, pad_e2)
    arrive_all(3, bricks(x1s, x1r), brick((x1,), lambda k, w, i: x1r[k, i]))

    def add(fine, x, j, up):
        x[j] = jnp.where(fine.inv[j] > 0.0, x[j] + up, 0.0)

    turn_by = lax.rem(yt - 4 * gy, yt)
    for i in range(12):
        v = pltpu.roll(e2pad[4 * gx + i], turn_by, 0)[0:12]
        up = refine_plane(v, 12, 24 * i, u128)
        add(l1, x1, 1 + 2 * i, up)
        add(l1, x1, 2 + 2 * i, up)
    e1, _ = l1.post(x1, y1, 3, 23, 1, steps(SMOOTH_LOWER, SMOOTH_UPPER, DEGREE))

    arrive_all(4, xstrips, place((x0,), ux, uy, uc))
    for i in range(12):
        up = refine_plane(e1[7 + i][6:18], 12, 24 * i, u256)
        add(l0, x0, 1 + 2 * i, up)
        add(l0, x0, 2 + 2 * i, up)
    r0, _ = l0.post(x0, y0, 1, 25, 1, steps(SMOOTH_LOWER, SMOOTH_UPPER, DEGREE))

    def give(i):
        out[i] = r0[1 + H + i, H : H + 16, :]

    loop(0, 16, give)
    sent_all(0, strips)
    sent_all(1, bricks(bc1s, bc1r))
    sent_all(2, bricks(f1s, f1r))
    sent_all(3, bricks(x1s, x1r))
    sent_all(4, xstrips)


def solution(mesh):
    nx_dev, ny_dev = mesh.shape["gx"], mesh.shape["gy"]
    n = nx_dev * ny_dev
    y2 = 4 * ny_dev

    def vm(*shape):
        return pltpu.VMEM(shape, F32)

    dims = [(26, 24, 256), (26, 24, 128)]
    for k in range(3):
        dims.append((2 + (4 * nx_dev >> k), max(8, y2 >> k), 128))
    shapes = []
    for d in dims:
        shapes += [vm(*d)] * 9 + [vm(6, *d)]
    shapes += [
        vm(max(12 * 24, 2 * nx_dev * y2), 128),
        vm(4 * nx_dev + 8, y2 + 8, 128),
        vm(8, 128),
        vm(16, 128),
        vm(n, 8, 128),
        vm(n, 16, 128),
    ]
    for count in (3, 3, 1, 1):
        shapes += [
            vm(2, count, H, 16, 256),
            vm(2, count, 16, H, 256),
            vm(4, count, H, H, 256),
        ]
    shapes += [vm(2, 8, 8, 128), vm(8, 2, 8, 8, 128)]
    shapes += [vm(8, 8, 128), vm(8, 8, 8, 128)] * 2
    shapes += [
        pltpu.SemaphoreType.DMA((5, 8)),
        pltpu.SemaphoreType.DMA((5, 8)),
        pltpu.SemaphoreType.DMA((2,)),
        pltpu.SemaphoreType.DMA((2,)),
    ]

    def per_device(source, conductivity, reaction):
        return pl.pallas_call(
            functools.partial(kernel, nx_dev, ny_dev),
            out_shape=jax.ShapeDtypeStruct(source.shape, F32),
            in_specs=[pl.BlockSpec(memory_space=pltpu.VMEM)] * 3,
            out_specs=pl.BlockSpec(memory_space=pltpu.VMEM),
            scratch_shapes=shapes,
            compiler_params=pltpu.CompilerParams(
                collective_id=0, has_side_effects=True, vmem_limit_bytes=48 << 20
            ),
        )(source, conductivity, reaction)

    spec = P("gx", "gy", None)
    return jax.shard_map(
        per_device, mesh=mesh, in_specs=(spec,) * 3, out_specs=spec, check_vma=False
    )
```

```python
import functools

import jax
import jax.numpy as jnp
from jax import lax
from jax.experimental import pallas as pl
from jax.experimental.pallas import tpu as pltpu
from jax.sharding import PartitionSpec as P

DEGREE = 4
BOTTOM = 8
SMOOTH_LOWER = 0.5
SMOOTH_UPPER = 2.0
BOTTOM_LOWER = 0.02

MESH = pl.DeviceIdType.MESH
F32 = jnp.float32
H = 4
DIRS = [(dx, dy) for dx in (-1, 0, 1) for dy in (-1, 0, 1) if (dx, dy) != (0, 0)]
DIRS.sort(key=lambda way: way[0] == 0)


def steps(lower, upper, count):
    center, half = 0.5 * (upper + lower), 0.5 * (upper - lower)
    q = center / half
    p = 1.0 / q
    out = [(0.0, 1.0 / center)]
    for _ in range(1, count):
        pn = 1.0 / (2.0 * q - p)
        out.append((pn * p, 2.0 * pn / half))
        p = pn
    return out


def loop(lo, hi, body, unroll=1):
    def step(i, carry):
        body(i)
        return carry

    lax.fori_loop(lo, hi, step, 0, unroll=unroll)


def planes(lo, hi, body, chunk):
    chunk = min(chunk, hi - lo)

    def group(i, size):
        stores = []
        for k in range(size):
            stores += body(i + k)
        for ref, index, value in stores:
            ref[index] = value

    whole = (hi - lo) // chunk
    if whole == 1:
        group(lo, chunk)
    else:
        loop(0, whole, lambda j: group(lo + j * chunk, chunk))
    if whole * chunk < hi - lo:
        group(lo + whole * chunk, hi - lo - whole * chunk)


def split_dot(v, m):
    hi = v.astype(jnp.bfloat16)
    lo = (v - hi.astype(F32)).astype(jnp.bfloat16)
    return jnp.dot(hi, m, preferred_element_type=F32) + jnp.dot(lo, m, preferred_element_type=F32)


def down_matrix(n):
    row = lax.broadcasted_iota(jnp.int32, (n, 128), 0)
    col = lax.broadcasted_iota(jnp.int32, (n, 128), 1)
    return jnp.where((row >= 2 * col) & (row < 2 * col + 2), 0.125, 0.0).astype(jnp.bfloat16)


def up_matrix(n):
    row = lax.broadcasted_iota(jnp.int32, (128, n), 0)
    col = lax.broadcasted_iota(jnp.int32, (128, n), 1)
    return jnp.where((col >= 2 * row) & (col < 2 * row + 2), 1.0, 0.0).astype(jnp.bfloat16)


class Level:
    def __init__(self, number, refs):
        self.s = 0.25**number
        self.f, self.b, self.c, self.x0, self.x1, self.d, self.g, self.inv, self.diag, self.w = refs
        self.nx, self.ny, self.nz = self.f.shape
        vregs = self.ny * self.nz // 1024
        self.chunk = max(2, 16 // vregs)

    def zero(self, *refs):
        z = jnp.zeros((self.ny, self.nz), F32)

        planes(0, self.nx, lambda i: [(r, i, z) for r in refs], self.chunk)

    def setup(self, lo, hi):
        ny, nz = self.ny, self.nz
        row = lax.broadcasted_iota(jnp.int32, (ny, nz), 0)
        col = lax.broadcasted_iota(jnp.int32, (ny, nz), 1)
        edges = (row == 0, row == ny - 1, col == 0, col == nz - 1)

        def body(i):
            b = self.b[i]
            c = self.c[i]
            near = [
                self.b[i - 1],
                self.b[i + 1],
                jnp.where(edges[0], 0.0, pltpu.roll(b, 1, 0)),
                jnp.where(edges[1], 0.0, pltpu.roll(b, ny - 1, 0)),
                jnp.where(edges[2], 0.0, pltpu.roll(b, 1, 1)),
                jnp.where(edges[3], 0.0, pltpu.roll(b, nz - 1, 1)),
            ]
            half = 0.5 * self.s
            faces = [half * (b + n) for n in near]
            diag = c
            for face in faces:
                diag = diag + face
            inside = c > 0.0
            inv = jnp.where(inside, 1.0 / jnp.where(inside, diag, 1.0), 0.0)
            stores = [(self.inv, i, inv), (self.diag, i, diag)]
            for k, face in enumerate(faces):
                w = face * inv
                if k >= 2:
                    w = jnp.where(edges[k - 2], 0.0, w)
                stores.append((self.w, (k, i), w))
            return stores

        planes(lo, hi, body, self.chunk)

    def start(self, lo, hi, b):
        def body(i):
            g = self.f[i] * self.inv[i]
            d = g * b
            return [(self.g, i, g), (self.d, i, d), (self.x0, i, d)]

        planes(lo, hi, body, self.chunk)

    def scaled_residual(self, x, i):
        v = x[i]
        t = self.g[i] - v
        t = t + self.w[0, i] * x[i - 1] + self.w[1, i] * x[i + 1]
        t = t + self.w[2, i] * pltpu.roll(v, 1, 0) + self.w[3, i] * pltpu.roll(v, self.ny - 1, 0)
        t = t + self.w[4, i] * pltpu.roll(v, 1, 1) + self.w[5, i] * pltpu.roll(v, self.nz - 1, 1)
        return v, t

    def sweep(self, x, y, a, b, lo, hi):
        def body(i):
            v, t = self.scaled_residual(x, i)
            d = b * t
            if a != 0.0:
                d = a * self.d[i] + d
            return [(self.d, i, d), (y, i, v + d)]

        planes(lo, hi, body, self.chunk)

    def pre(self, lo, hi, shrink, pairs):
        self.start(lo, hi, pairs[0][1])
        x, y = self.x0, self.x1
        for a, b in pairs[1:]:
            lo, hi = lo + shrink, hi - shrink
            self.sweep(x, y, a, b, lo, hi)
            x, y = y, x
        return x, y

    def post(self, x, y, lo, hi, shrink, pairs):
        for a, b in pairs:
            lo, hi = lo + shrink, hi - shrink
            self.sweep(x, y, a, b, lo, hi)
            x, y = y, x
        return x, y

    def coarse_residual(self, x, first, count, m, scratch):
        def body(i):
            j = first + 2 * i
            _, t0 = self.scaled_residual(x, j)
            _, t1 = self.scaled_residual(x, j + 1)
            v = self.diag[j] * t0 + self.diag[j + 1] * t1
            scratch[i * self.ny : (i + 1) * self.ny, :] = split_dot(v, m)

        for i in range(count):
            body(i)


def coarse_array(ref, first, count, m, scratch):
    ny = ref.shape[1]
    for i in range(count):
        v = ref[first + 2 * i] + ref[first + 2 * i + 1]
        scratch[i * ny : (i + 1) * ny, :] = split_dot(v, m)


def pairs_of(scratch, start, size):
    return scratch[pl.ds(start, size, stride=2), :] + scratch[pl.ds(start + 1, size, stride=2), :]


def kernel(
    nx_dev, ny_dev, f_in, b_in, c_in, out, *refs
):
    refs = list(refs)

    def take(n):
        got = refs[:n]
        del refs[:n]
        return got

    levels = [Level(k, take(10)) for k in range(5)]
    l0, l1, l2, l3, l4 = levels
    scratch, e2pad, f2s, bc2s, f2l, bc2l = take(6)
    sx, sy, sc, rx, ry, rc = take(6)
    tx, ty, tc, ux, uy, uc = take(6)
    bc1s, bc1r, f1s, f1r, x1s, x1r = take(6)
    ssem, rsem, gssem, grsem = take(4)

    gx = lax.axis_index("gx")
    gy = lax.axis_index("gy")
    n = nx_dev * ny_dev
    me = gx * ny_dev + gy
    m256, m128 = down_matrix(256), down_matrix(128)
    u256, u128 = up_matrix(256), up_matrix(128)

    barrier = pltpu.get_barrier_semaphore()

    def greet(k):
        t = lax.rem(me + k, n)
        pl.semaphore_signal(
            barrier, inc=1, device_id=(t // ny_dev, lax.rem(t, ny_dev)), device_id_type=MESH
        )

    loop(1, n, greet)

    def present(dx, dy):
        ok = None
        for delta, at, size in ((dx, gx, nx_dev), (dy, gy, ny_dev)):
            if delta == 1:
                cond = at < size - 1
            elif delta == -1:
                cond = at > 0
            else:
                continue
            ok = cond if ok is None else ok & cond
        return ok

    def neighbour_copy(k, turn, src, dst):
        dx, dy = DIRS[k]
        return pltpu.make_async_remote_copy(
            src_ref=src,
            dst_ref=dst,
            send_sem=ssem.at[turn, k],
            recv_sem=rsem.at[turn, k],
            device_id=(gx + dx, gy + dy),
            device_id_type=MESH,
        )

    def slot(k, xs, ys, cs):
        dx, dy = DIRS[k]
        if dy == 0:
            return xs.at[(dx + 1) // 2]
        if dx == 0:
            return ys.at[(dy + 1) // 2]
        return cs.at[(dx + 1) + (dy + 1) // 2]

    def send_all(turn, pair_of):
        for k, (dx, dy) in enumerate(DIRS):

            @pl.when(present(dx, dy))
            def _():
                neighbour_copy(k, turn, *pair_of(k)).start()

    def arrive_all(turn, pair_of, use, want=lambda dx: True):
        for k, (dx, dy) in enumerate(DIRS):
            if not want(dx):
                continue

            @pl.when(present(-dx, -dy))
            def _():
                neighbour_copy(k, turn, *pair_of(k)).wait_recv()
                use(k, dx, dy)

    def sent_all(turn, pair_of):
        for k, (dx, dy) in enumerate(DIRS):

            @pl.when(present(dx, dy))
            def _():
                neighbour_copy(k, turn, *pair_of(k)).wait_send()

    def source_span(delta):
        if delta == 0:
            return 0, 16, None, None
        return (16 - H, H, 16 - H, 15 - H) if delta == 1 else (0, H, H - 1, H)

    def landing(delta):
        return {0: (H, 16), 1: (0, H), -1: (H + 16, H)}[delta]

    for k, (dx, dy) in enumerate(DIRS):
        buf = slot(k, sx, sy, sc)
        px, cx, ox, beyx = source_span(dx)
        py, cy, oy, beyy = source_span(dy)
        for which, ref in enumerate((f_in, b_in, c_in)):

            def body(i, which=which, ref=ref, buf=buf, px=px, py=py, cy=cy):
                return [(buf, (which, i), ref[px + i, py : py + cy, :])]

            planes(0, cx, body, 4)
        if dx != 0:
            i = ox - px
            buf[2, i] = buf[2, i] + 0.5 * b_in[beyx, py : py + cy, :]
        if dy != 0:

            def edge(i, buf=buf, px=px, py=py, oy=oy, beyy=beyy):
                buf[2, i, oy - py : oy - py + 1, :] = (
                    buf[2, i, oy - py : oy - py + 1, :] + 0.5 * b_in[px + i, beyy : beyy + 1, :]
                )

            loop(0, cx, edge)

    pl.semaphore_wait(barrier, n - 1)

    strips = lambda k: (slot(k, sx, sy, sc), slot(k, rx, ry, rc))
    bricks = lambda s, r: (lambda k: (s, r.at[k]))
    send_all(0, strips)

    bc1 = []
    for which, ref in enumerate((b_in, c_in)):
        coarse_array(ref, 0, 8, m256, scratch)
        for i in range(8):
            bc1s[which, i] = pairs_of(scratch, 16 * i, 8)
    half = []
    for which in range(2):
        coarse_array(bc1s.at[which], 0, 4, m128, scratch)
        half.append(
            jnp.concatenate([pairs_of(scratch, 8 * i, 4) for i in range(4)], axis=0)
        )
    bc2s[...] = half[0] + pltpu.roll(half[1], 64, 1)

    def gather_start(turn, src, dst):
        dst[me] = src[...]

        def body(k):
            t = lax.rem(me + k, n)
            pltpu.make_async_remote_copy(
                src_ref=src,
                dst_ref=dst.at[me],
                send_sem=gssem.at[turn],
                recv_sem=grsem.at[turn],
                device_id=(t // ny_dev, lax.rem(t, ny_dev)),
                device_id_type=MESH,
            ).start()

        loop(1, n, body)

    def gather_wait(turn, dst):
        whole = dst.at[pl.ds(0, n - 1)]
        other = lax.rem(me + 1, n)
        copy = pltpu.make_async_remote_copy(
            src_ref=whole,
            dst_ref=whole,
            send_sem=gssem.at[turn],
            recv_sem=grsem.at[turn],
            device_id=(other // ny_dev, lax.rem(other, ny_dev)),
            device_id_type=MESH,
        )
        copy.wait_send()
        copy.wait_recv()


    l0.zero(l0.f, l0.b, l0.c)

    def inner(i):
        return [
            (dst, (i + 1 + H, slice(H, H + 16)), src[i])
            for dst, src in ((l0.f, f_in), (l0.b, b_in), (l0.c, c_in))
        ]

    planes(0, 16, inner, 2)

    def place(dsts, xs, ys, cs):
        def use(k, dx, dy):
            buf = slot(k, xs, ys, cs)
            px, cx = landing(dx)
            py, cy = landing(dy)

            def body(i):
                return [
                    (dst, (1 + px + i, slice(py, py + cy)), buf[which, i])
                    for which, dst in enumerate(dsts)
                ]

            planes(0, cx, body, 4)

        return use

    landed = place((l0.f, l0.b, l0.c), rx, ry, rc)
    arrive_all(0, strips, landed, lambda dx: dx == 0)
    smoothing = steps(SMOOTH_LOWER, SMOOTH_UPPER, DEGREE)
    l0.setup(6, 20)
    x0, y0 = l0.pre(6, 20, 1, smoothing)
    arrive_all(0, strips, landed, lambda dx: dx != 0)
    send_all(1, bricks(bc1s, bc1r))
    gather_start(0, bc2s, bc2l)
    l0.setup(1, 6)
    l0.setup(20, 25)
    l0.start(1, 6, smoothing[0][1])
    l0.start(20, 25, smoothing[0][1])
    now, later = l0.x0, l0.x1
    for k in range(1, DEGREE):
        a, b = smoothing[k]
        l0.sweep(now, later, a, b, 1 + k, 6 + k)
        l0.sweep(now, later, a, b, 20 - k, 25 - k)
        now, later = later, now
    l0.coarse_residual(x0, 1 + H, 8, m256, scratch)
    for i in range(8):
        f1s[i] = pairs_of(scratch, 24 * i + H, 8)
    send_all(2, bricks(f1s, f1r))

    for k, (dx, dy) in enumerate(DIRS):
        buf = slot(k, tx, ty, tc)
        px, cx, _, _ = source_span(dx)
        py, cy, _, _ = source_span(dy)

        def body(i, buf=buf, px=px, py=py, cy=cy):
            return [(buf, (0, i), x0[1 + H + px + i, H + py : H + py + cy, :])]

        planes(0, cx, body, 4)
    xstrips = lambda k: (slot(k, tx, ty, tc), slot(k, ux, uy, uc))

    l1.zero(l1.f, l1.b, l1.c)

    def brick(dsts, src):
        def use(k, dx, dy):
            for which, dst in enumerate(dsts):
                for i in range(8):
                    dst[9 - 8 * dx + i, 8 - 8 * dy : 16 - 8 * dy, :] = src(k, which, i)

        return use

    for i in range(8):
        l1.b[9 + i, 8:16, :] = bc1s[0, i]
        l1.c[9 + i, 8:16, :] = bc1s[1, i]
        l1.f[9 + i, 8:16, :] = f1s[i]
    arrive_all(1, bricks(bc1s, bc1r), brick((l1.b, l1.c), lambda k, w, i: bc1r[k, w, i]))
    l1.setup(1, 25)
    arrive_all(2, bricks(f1s, f1r), brick((l1.f,), lambda k, w, i: f1r[k, i]))
    x1, y1 = l1.pre(1, 25, 1, steps(SMOOTH_LOWER, SMOOTH_UPPER, DEGREE))
    l1.coarse_residual(x1, 9, 4, m128, scratch)
    f2 = [pairs_of(scratch, 24 * i + 8, 4) for i in range(4)]
    f2s[...] = jnp.concatenate(f2[:2], axis=0) + pltpu.roll(
        jnp.concatenate(f2[2:], axis=0), 64, 1
    )
    gather_start(1, f2s, f2l)
    for i in range(8):
        x1s[i] = x1[9 + i, 8:16, :]
    send_all(3, bricks(x1s, x1r))
    send_all(4, xstrips)

    for lv in (l2, l3, l4):
        lv.zero(lv.f, lv.b, lv.c, lv.x0, lv.x1)
    gather_wait(0, bc2l)

    def low(v):
        col = lax.broadcasted_iota(jnp.int32, v.shape, 1)
        return jnp.where(col < 64, v, 0.0)

    def spread_bc(a):
        for e in range(ny_dev):
            v = bc2l[a * ny_dev + e]
            b2, c2 = low(v), low(pltpu.roll(v, 64, 1))
            for i in range(4):
                l2.b[1 + 4 * a + i, 4 * e : 4 * e + 4, :] = b2[4 * i : 4 * i + 4]
                l2.c[1 + 4 * a + i, 4 * e : 4 * e + 4, :] = c2[4 * i : 4 * i + 4]

    loop(0, nx_dev, spread_bc)
    for fine, coarse in ((l2, l3), (l3, l4)):
        nxc, nyc = (fine.nx - 2) // 2, fine.ny // 2
        for src, dst in ((fine.b, coarse.b), (fine.c, coarse.c)):
            coarse_array(src, 1, nxc, m128, scratch)
            for i in range(nxc):
                dst[1 + i, 0:nyc, :] = pairs_of(scratch, fine.ny * i, nyc)
    for lv in (l2, l3, l4):
        lv.setup(1, lv.nx - 1)

    gather_wait(1, f2l)

    def spread_f(a):
        for e in range(ny_dev):
            v = f2l[a * ny_dev + e]
            p01, p23 = low(v), low(pltpu.roll(v, 64, 1))
            for i in range(4):
                p = (p01, p23)[i // 2]
                r = 4 * (i % 2)
                l2.f[1 + 4 * a + i, 4 * e : 4 * e + 4, :] = p[r : r + 4]

    loop(0, nx_dev, spread_f)
    found = []
    for fine, coarse in ((l2, l3), (l3, l4)):
        x, y = fine.pre(1, fine.nx - 1, 0, steps(SMOOTH_LOWER, SMOOTH_UPPER, DEGREE))
        found.append((x, y))
        nxc, nyc = (fine.nx - 2) // 2, fine.ny // 2
        fine.coarse_residual(x, 1, nxc, m128, scratch)
        for i in range(nxc):
            coarse.f[1 + i, 0:nyc, :] = pairs_of(scratch, fine.ny * i, nyc)
    e, _ = l4.pre(1, l4.nx - 1, 0, steps(BOTTOM_LOWER, SMOOTH_UPPER, BOTTOM))

    def refine_plane(v, rows, at, u):
        scratch[pl.ds(at, rows, stride=2), :] = v
        scratch[pl.ds(at + 1, rows, stride=2), :] = v
        return split_dot(scratch[at : at + 2 * rows, :], u)

    for fine, coarse, (x, y) in ((l3, l4, found[1]), (l2, l3, found[0])):
        nxc, nyc = (fine.nx - 2) // 2, fine.ny // 2
        for i in range(nxc):
            up = refine_plane(e[1 + i][0:nyc], nyc, i * fine.ny, u128)
            x[1 + 2 * i] = x[1 + 2 * i] + up
            x[2 + 2 * i] = x[2 + 2 * i] + up
        e, _ = fine.post(x, y, 1, fine.nx - 1, 0, steps(SMOOTH_LOWER, SMOOTH_UPPER, DEGREE))

    yt = e2pad.shape[1]
    zero_plane = jnp.zeros((yt, 128), F32)

    def clear(i):
        e2pad[i] = zero_plane

    loop(0, e2pad.shape[0], clear)

    def pad_e2(i):
        e2pad[4 + i, 4 : 4 + l2.ny, :] = e[1 + i]

    loop(0, l2.nx - 2, pad_e2)
    arrive_all(3, bricks(x1s, x1r), brick((x1,), lambda k, w, i: x1r[k, i]))

    def add(fine, x, j, up):
        x[j] = jnp.where(fine.inv[j] > 0.0, x[j] + up, 0.0)

    turn_by = lax.rem(yt - 4 * gy, yt)
    for i in range(12):
        v = pltpu.roll(e2pad[4 * gx + i], turn_by, 0)[0:12]
        up = refine_plane(v, 12, 24 * i, u128)
        add(l1, x1, 1 + 2 * i, up)
        add(l1, x1, 2 + 2 * i, up)
    e1, _ = l1.post(x1, y1, 3, 23, 1, steps(SMOOTH_LOWER, SMOOTH_UPPER, DEGREE))

    arrive_all(4, xstrips, place((x0,), ux, uy, uc))
    for i in range(12):
        up = refine_plane(e1[7 + i][6:18], 12, 24 * i, u256)
        add(l0, x0, 1 + 2 * i, up)
        add(l0, x0, 2 + 2 * i, up)
    r0, _ = l0.post(x0, y0, 1, 25, 1, steps(SMOOTH_LOWER, SMOOTH_UPPER, DEGREE))

    def give(i):
        return [(out, i, r0[1 + H + i, H : H + 16, :])]

    planes(0, 16, give, 4)
    sent_all(0, strips)
    sent_all(1, bricks(bc1s, bc1r))
    sent_all(2, bricks(f1s, f1r))
    sent_all(3, bricks(x1s, x1r))
    sent_all(4, xstrips)


def solution(mesh):
    nx_dev, ny_dev = mesh.shape["gx"], mesh.shape["gy"]
    n = nx_dev * ny_dev
    y2 = 4 * ny_dev

    def vm(*shape):
        return pltpu.VMEM(shape, F32)

    dims = [(26, 24, 256), (26, 24, 128)]
    for k in range(3):
        dims.append((2 + (4 * nx_dev >> k), max(8, y2 >> k), 128))
    shapes = []
    for d in dims:
        shapes += [vm(*d)] * 9 + [vm(6, *d)]
    shapes += [
        vm(max(12 * 24, 2 * nx_dev * y2), 128),
        vm(4 * nx_dev + 8, y2 + 8, 128),
        vm(8, 128),
        vm(16, 128),
        vm(n, 8, 128),
        vm(n, 16, 128),
    ]
    for count in (3, 3, 1, 1):
        shapes += [
            vm(2, count, H, 16, 256),
            vm(2, count, 16, H, 256),
            vm(4, count, H, H, 256),
        ]
    shapes += [vm(2, 8, 8, 128), vm(8, 2, 8, 8, 128)]
    shapes += [vm(8, 8, 128), vm(8, 8, 8, 128)] * 2
    shapes += [
        pltpu.SemaphoreType.DMA((5, 8)),
        pltpu.SemaphoreType.DMA((5, 8)),
        pltpu.SemaphoreType.DMA((2,)),
        pltpu.SemaphoreType.DMA((2,)),
    ]

    def per_device(source, conductivity, reaction):
        return pl.pallas_call(
            functools.partial(kernel, nx_dev, ny_dev),
            out_shape=jax.ShapeDtypeStruct(source.shape, F32),
            in_specs=[pl.BlockSpec(memory_space=pltpu.VMEM)] * 3,
            out_specs=pl.BlockSpec(memory_space=pltpu.VMEM),
            scratch_shapes=shapes,
            compiler_params=pltpu.CompilerParams(
                collective_id=0, has_side_effects=True, vmem_limit_bytes=48 << 20
            ),
        )(source, conductivity, reaction)

    spec = P("gx", "gy", None)
    return jax.shard_map(
        per_device, mesh=mesh, in_specs=(spec,) * 3, out_specs=spec, check_vma=False
    )
```
